32 devices in a mesh: seq: 8 (over z, x), exp: 4 (over y, core).
Axes of the slice: x: 2, y: 2, z: 4, core: 2. Of those that a mesh axis runs over, the one named last changes fastest.
Arguments:
- projected: bfloat16 [4, 1024, 3, 4096], P('exp', 'seq'), may hold values from -8 to 8
- patches: bfloat16 [4, 1024, 4096], P('exp', 'seq'), may hold values from -6 to 6
- norm_gain: float32 [4096], replicated, may hold values from 0.1 to 1.9
- expert_ids: int32 [4, 1024, 2], P('exp', 'seq'), may hold values from 0 to 31, all different within a row; in each aligned block of 128 rows (0 to 127, 128 to 255, ..., all dimensions but the last counted through in order) at most 16 rows name the same one
- gate_levels: int32 [4, 1024, 2], P('exp', 'seq'), may hold values from 1 to 256
- w_gate: bfloat16 [32, 4096, 768], P(('seq', 'exp')), may hold values from -0.09375 to 0.09375
- w_up: bfloat16 [32, 4096, 768], P(('seq', 'exp')), may hold values from -0.09375 to 0.09375
- w_down: bfloat16 [32, 768, 4096], P(('seq', 'exp')), may hold values from -0.21875 to 0.21875
Outputs:
- attended: bfloat16 [4, 1024, 4096], P('exp', 'seq')
- layer_out: bfloat16 [4, 1024, 4096], P('exp', 'seq')
The draws below stay inside these ranges and needn't reach their ends.
Inputs may be any that keep to these rules, and one draw needn't show every extreme that they name: `expert_ids`: each patch names two different experts. Among the 128 patches of one device (aligned blocks of rows, sequences first), at most 16 name the same expert, and in every draw some expert is named by exactly 16 patches of some device.
All inputs are finite; a program needn't handle non-finite values.
Results may differ from the reference program's by a relative error of at most 0.0068.
Values may be sent and summed in bfloat16 or wider, within the bound.
No kernel may reach another device: no remote copies, remote signals or barrier semaphores. Data moves between devices by JAX's collectives and lax.ppermute only.
A program may use at most 128 MiB of HBM per device.

```python
import math
import jax
import jax.numpy as jnp
import numpy as np
from jax import lax

D = 4096
HEADS = 32
FFW = 768
TOK_DEV = 128
HEAD_DIM = 128
LENGTH = 1024
SEQS = 4
EXPERTS = 32
CAP = 16
N_SEQ = 8


def draw_projected(key, part):
    first_key = jax.random.fold_in(key, 0)
    shape = (SEQS, LENGTH, 3, D)
    which = lax.broadcasted_iota(jnp.int32, shape, 2)
    normal_part = jax.random.normal(first_key, shape, jnp.float32)
    values = jnp.clip(jnp.where(which == 2, 2.0 * normal_part, 1.3 * normal_part), -8.0, 8.0)
    return values.astype(jnp.bfloat16)


def set_ends(result, stream_key, least, top_value):
    longest = result.shape.index(max(result.shape))
    spots = []
    for shift in (0, 1):
        where = [jax.random.randint(jax.random.fold_in(stream_key, axis), (), 0, length) for axis, length in enumerate(result.shape)]
        where[longest] = (where[longest] + shift) % result.shape[longest]
        spots.append(tuple(where))
    return result.at[spots[0]].set(least).at[spots[1]].set(top_value)


def level_of(own_key, shape, shards, least, top_value):
    loudness, own = 1.0, jax.random.fold_in(own_key, 6)
    for dim, shards_of in shards:
        draws = jnp.exp(jax.random.uniform(jax.random.fold_in(own, dim), (shards_of,), jnp.float32, least / len(shards), top_value / len(shards)))
        loudness = loudness * jnp.repeat(draws, shape[dim] // shards_of).reshape([-1 if axis == dim else 1 for axis in range(len(shape))])
    return loudness


def deal_out(own_key, own, number, rows, number_of, top, limit, slope):
    ranking = jax.random.permutation(own_key, number_of)
    crowded, usual = portions_of(number_of, rows * top, limit, slope, True), portions_of(number_of, rows * top, limit, slope, False)
    places = jnp.arange(number_of)

    def named(tallies, turn):
        used = int((tallies > 0).sum())
        fixed = max(1, used // 4)
        passed = fixed + (places - fixed + turn * (used - fixed)) % max(1, number_of - fixed)
        return jnp.zeros((number_of,), jnp.int32).at[ranking[jnp.where(places < fixed, places, passed)]].set(jnp.asarray(tallies, jnp.int32))

    tallies = jnp.where(number % 4 == 0, named(crowded, number // 4), named(usual, number - number // 4 - 1))
    mixed = jax.random.permutation(jax.random.fold_in(own, 3), number_of)
    source_of, taker = mixed[0:number_of // 2 * 2:2], mixed[1:number_of // 2 * 2:2]
    room = jnp.minimum(tallies[source_of] - 1, limit - tallies[taker]) // 2
    room = jnp.where((source_of == ranking[0]) | (taker == ranking[0]) | (tallies[taker] == 0), 0, jnp.maximum(room, 0))
    passed = jax.random.randint(jax.random.fold_in(own, 4), (number_of // 2,), 0, 1 << 20) % (room + 1)
    tallies = tallies.at[source_of].add(-passed).at[taker].add(passed)
    members = jnp.searchsorted(jnp.cumsum(tallies), jnp.arange(rows * top), side="right").astype(jnp.int32)
    grid = members.reshape(top, rows).T
    grid = grid[jax.random.permutation(jax.random.fold_in(own, 1), rows)]
    turn = jax.random.randint(jax.random.fold_in(own, 2), (rows, 1), 0, top)
    return jnp.take_along_axis(grid, (jnp.arange(top)[None, :] + turn) % top, axis=1)


def portions_of(amount, total, limit, lean, full):
    loads = [(1 << 20) // math.isqrt(standing ** lean) + 1 for standing in range(1, amount + 1)]
    largest = limit if full else min(limit, max(-(-total // amount), total * loads[0] // sum(loads)))
    least = 1 if total - largest >= amount - 1 else 0
    given, surplus = [largest] + [least] * (amount - 1), total - largest - least * (amount - 1)
    while surplus > 0:
        free = [i for i in range(1, amount) if given[i] < largest] or [i for i in range(1, amount) if given[i] < limit]
        pool, budget = sum([loads[i] for i in free]), surplus
        for i in free:
            addition = min(limit - given[i], max(1, budget * loads[i] // pool), surplus)
            given[i] = given[i] + addition
            surplus = surplus - addition
    return np.array(given)


def noise(own_key, extent, spread, reach, cuts=(), kind=jnp.bfloat16):
    drawn = jax.random.normal(own_key, extent, jnp.float32) * spread
    if len(cuts) > 0:
        drawn = level_of(own_key, extent, cuts, -0.22, 0.18) * drawn
    return jnp.clip(drawn, min=-reach, max=reach).astype(kind)


def setup_inputs(seed: int = 0) -> dict:
    keys = jax.random.split(jax.random.key(seed), 9)
    projected = draw_projected(jax.random.fold_in(keys[8], 71), 0)
    patches = noise(keys[1], (SEQS, LENGTH, D), 1.0, 6.0, ((0, 4), (1, 8)))
    norm_gain = jnp.clip(1.0 + 0.18 * jax.random.normal(keys[2], (D,), jnp.float32), 0.1, 1.9)
    expert_ids_keys = jax.random.split(jax.random.fold_in(keys[3], 1), SEQS * LENGTH // TOK_DEV)
    expert_ids_turns = jax.random.permutation(jax.random.fold_in(keys[3], 3), SEQS * LENGTH // TOK_DEV)
    expert_ids = jax.vmap(lambda own, number: deal_out(jax.random.fold_in(keys[3], 2), own, number, TOK_DEV, EXPERTS, 2, CAP, 2))(expert_ids_keys, expert_ids_turns).reshape((SEQS, LENGTH, 2))
    gate_levels = set_ends(jax.random.randint(keys[4], (SEQS, LENGTH, 2), 1, 257), jax.random.fold_in(keys[4], 1), 1, 256).astype(jnp.int32)
    w_gate = noise(keys[5], (EXPERTS, D, FFW), D ** -0.5, 0.09375, ((0, 32),))
    w_up = noise(keys[6], (EXPERTS, D, FFW), D ** -0.5, 0.09375, ((0, 32),))
    w_down = noise(keys[7], (EXPERTS, FFW, D), FFW ** -0.5, 0.21875, ((0, 32),))
    return dict(projected=projected, patches=patches, norm_gain=norm_gain, expert_ids=expert_ids, gate_levels=gate_levels, w_gate=w_gate, w_up=w_up, w_down=w_down)


def one_head(member):
    query_rows, key_rows, value_rows = member
    scale = 1.0 / math.sqrt(HEAD_DIM)
    scores = jnp.dot(query_rows, key_rows.T, preferred_element_type=jnp.float32) * scale
    query_pos = lax.broadcasted_iota(jnp.int32, (LENGTH, LENGTH), 0)
    key_pos = lax.broadcasted_iota(jnp.int32, (LENGTH, LENGTH), 1)
    scores = jnp.where(key_pos <= query_pos, scores, jnp.float32(-1e+30))
    highest = lax.optimization_barrier(jnp.max(scores, axis=-1, keepdims=True))
    weights = jnp.exp(scores - highest)
    probs = (weights / lax.optimization_barrier(jnp.sum(weights, axis=-1, keepdims=True))).astype(jnp.bfloat16)
    return jnp.dot(probs, value_rows, preferred_element_type=jnp.float32).astype(jnp.bfloat16)

def one_expert(member):
    arrived, gate_mat, up_mat, down_mat = member
    gate_part = jnp.dot(arrived, gate_mat, preferred_element_type=jnp.float32)
    up_part = jnp.dot(arrived, up_mat, preferred_element_type=jnp.float32)
    hidden = (jax.nn.silu(gate_part) * up_part).astype(jnp.bfloat16)
    return jnp.dot(hidden, down_mat, preferred_element_type=jnp.float32).astype(jnp.bfloat16)

def reference(projected, patches, norm_gain, expert_ids, gate_levels, w_gate, w_up, w_down):
    split_heads = projected.reshape(SEQS, LENGTH, 3, HEADS, HEAD_DIM)
    stacked = jnp.transpose(split_heads, (2, 0, 3, 1, 4)).reshape(3, SEQS * HEADS, LENGTH, HEAD_DIM)
    head_out = lax.map(one_head, (stacked[0], stacked[1], stacked[2]))
    attended = jnp.transpose(head_out.reshape(SEQS, HEADS, LENGTH, HEAD_DIM), (0, 2, 1, 3)).reshape(SEQS, LENGTH, D)
    stream = (patches.astype(jnp.float32) + attended.astype(jnp.float32)).astype(jnp.bfloat16)
    stream_f = stream.astype(jnp.float32)
    mean_square = lax.optimization_barrier(jnp.mean(stream_f * stream_f, axis=-1, keepdims=True))
    normed = (stream_f * lax.rsqrt(mean_square + 1e-05) * norm_gain.astype(jnp.float32)).astype(jnp.bfloat16)
    blocks = SEQS * N_SEQ
    routed = expert_ids.reshape(blocks, 2 * TOK_DEV).astype(jnp.int32)
    onehot = (routed[:, :, None] == jnp.arange(EXPERTS, dtype=jnp.int32)[None, None, :]).astype(jnp.int32)
    slot = lax.optimization_barrier(jnp.sum(jnp.cumsum(onehot, axis=1) * onehot, axis=2)) - 1
    block_index = jnp.arange(blocks, dtype=jnp.int32)[:, None]
    target = (routed * (blocks * CAP) + block_index * CAP + slot).reshape(-1).astype(jnp.int32)
    source_rows = jnp.repeat(normed.reshape(blocks * TOK_DEV, D), 2, axis=0)
    buffer = jnp.zeros((EXPERTS * blocks * CAP, D), jnp.bfloat16).at[target].set(source_rows)
    results = lax.map(one_expert, (buffer.reshape(EXPERTS, blocks * CAP, D), w_gate, w_up, w_down))
    picked = results.reshape(EXPERTS * blocks * CAP, D)[target].reshape(SEQS, LENGTH, 2, D).astype(jnp.float32)
    levels = gate_levels.astype(jnp.float32)
    share = levels / lax.optimization_barrier(jnp.sum(levels, axis=-1, keepdims=True))
    mixture = picked[:, :, 0, :] * share[:, :, 0:1] + picked[:, :, 1, :] * share[:, :, 1:2]
    layer_out = (stream_f + mixture).astype(jnp.bfloat16)
    return (attended, layer_out)
```

```python
import functools
import math

import jax
import jax.numpy as jnp
from jax import lax
from jax.experimental import pallas as pl
from jax.experimental.pallas import tpu as pltpu
from jax.sharding import Mesh
from jax.sharding import PartitionSpec as P

HEADS = 32
SEQ = ("hi", "lo")
HALF = ("lo", "exp")
BF = jnp.bfloat16
F32 = jnp.float32


def attention_kernel(step_rows, qkv_ref, out_ref):
    blocks, _, rows, head_width = qkv_ref.shape
    length = blocks * rows
    factor = math.log2(math.e) / math.sqrt(head_width)
    queries = qkv_ref[:, 0].reshape(length, head_width)
    keys = qkv_ref[:, 1].reshape(length, head_width)
    values = qkv_ref[:, 2].reshape(length, head_width)
    over_width = (((1,), (1,)), ((), ()))
    shape = (step_rows, step_rows)
    seen = lax.broadcasted_iota(jnp.int32, shape, 1) <= lax.broadcasted_iota(jnp.int32, shape, 0)
    for start in range(0, length, step_rows):
        stop = start + step_rows
        part = queries[start:stop]
        near = lax.dot_general(part, keys[start:stop], over_width, preferred_element_type=F32)
        near = jnp.where(seen, near, F32(-1e30))
        highest = jnp.max(near, axis=-1, keepdims=True)
        if start:
            far = lax.dot_general(part, keys[:start], over_width, preferred_element_type=F32)
            highest = jnp.maximum(highest, jnp.max(far, axis=-1, keepdims=True))
        near = jnp.exp2((near - highest) * factor)
        total = jnp.sum(near, axis=-1, keepdims=True)
        mixed = jnp.dot(near.astype(BF), values[start:stop], preferred_element_type=F32)
        if start:
            far = jnp.exp2((far - highest) * factor)
            total += jnp.sum(far, axis=-1, keepdims=True)
            mixed += jnp.dot(far.astype(BF), values[:start], preferred_element_type=F32)
        mixed = (mixed / total).astype(BF)
        for block in range(start // rows, stop // rows):
            low = block * rows - start
            out_ref[block] = mixed[low : low + rows]


def attention(arrived, local_heads):
    blocks, _, rows, local_width = arrived.shape
    head_width = local_width // local_heads
    length = blocks * rows
    return pl.pallas_call(
        functools.partial(attention_kernel, 2 * rows),
        grid=(local_heads,),
        in_specs=[pl.BlockSpec((blocks, 3, rows, head_width), lambda head: (0, 0, 0, head))],
        out_specs=pl.BlockSpec((blocks, rows, head_width), lambda head: (0, 0, head)),
        out_shape=jax.ShapeDtypeStruct((blocks, rows, local_width), BF),
        cost_estimate=pl.CostEstimate(
            flops=2 * length * length * local_width,
            bytes_accessed=8 * length * local_width,
            transcendentals=length * length * local_heads // 2,
        ),
    )(arrived)


def expert_ffn(arrived, w_gate, w_up, w_down):
    rows = arrived.reshape(-1, arrived.shape[-1])
    gate_part = jnp.dot(rows, w_gate[0], preferred_element_type=F32)
    up_part = jnp.dot(rows, w_up[0], preferred_element_type=F32)
    hidden = (jax.nn.silu(gate_part) * up_part).astype(BF)
    result = jnp.dot(hidden, w_down[0], preferred_element_type=F32).astype(BF)
    return result.reshape(arrived.shape)


def routing(expert_ids, gate_levels, first, experts, capacity):
    rows = expert_ids.shape[0]
    routed = expert_ids.reshape(-1)
    names = lax.broadcasted_iota(jnp.int32, (2 * rows, 2 * rows), 1)
    same = (routed[:, None] == routed[None, :]) & (
        names < lax.broadcasted_iota(jnp.int32, (2 * rows, 2 * rows), 0)
    )
    slot = jnp.sum(same.astype(jnp.int32), axis=1)
    local = routed - first
    position = jnp.where((local >= 0) & (local < experts), local * capacity + slot, -1)
    position = position.reshape(rows, 2)
    levels = gate_levels.astype(F32)
    share = levels / jnp.sum(levels, axis=-1, keepdims=True)
    places = lax.broadcasted_iota(jnp.int32, (rows, experts * capacity), 1)
    hit0 = places == position[:, 0:1]
    hit1 = places == position[:, 1:2]
    send = (hit0 | hit1).astype(BF)
    weight = jnp.where(hit0, share[:, 0:1], F32(0)) + jnp.where(hit1, share[:, 1:2], F32(0))
    high = lax.reduce_precision(weight, 8, 7)
    return send, high.astype(BF), (weight - high).astype(BF)


def spread(send, rows):
    return lax.dot_general(
        send, rows, (((0,), (0,)), ((), ())), preferred_element_type=F32
    ).astype(BF)


def gather_back(high, low, rows):
    return jnp.dot(high, rows, preferred_element_type=F32) + jnp.dot(
        low, rows, preferred_element_type=F32
    )


def shards(projected, patches, norm_gain, expert_ids, gate_levels, w_gate, w_up, w_down):
    seq_count = lax.axis_size(SEQ)
    half_count = lax.axis_size(HALF)
    lo_count = lax.axis_size("lo")
    tok_rows = patches.shape[1]
    width = patches.shape[2]
    local_width = width // seq_count
    local_heads = HEADS // seq_count
    expert_count = 2 * half_count
    capacity = max(2, 4 * tok_rows // expert_count)
    mirror = [(i, (i + lo_count) % seq_count) for i in range(seq_count)]
    first = lax.axis_index("hi") * half_count

    def across(value):
        return lax.ppermute(value, SEQ, mirror)

    def exchange(value):
        return lax.all_to_all(value, HALF, split_axis=0, concat_axis=0, tiled=True)

    other_ids = across(expert_ids[0])
    other_levels = across(gate_levels[0])
    own_send, own_high, own_low = routing(
        expert_ids[0], gate_levels[0], first, half_count, capacity
    )
    other_send, other_high, other_low = routing(
        other_ids, other_levels, first, half_count, capacity
    )

    outgoing = jnp.transpose(
        projected[0].reshape(tok_rows, 3, seq_count, local_width), (2, 1, 0, 3)
    )
    arrived = lax.all_to_all(outgoing, SEQ, split_axis=0, concat_axis=0, tiled=True)
    mixed = attention(arrived, local_heads)
    returned = lax.all_to_all(mixed, SEQ, split_axis=0, concat_axis=0, tiled=True)
    attended = jnp.transpose(returned, (1, 0, 2)).reshape(tok_rows, width)
    stream = (patches[0].astype(F32) + attended.astype(F32)).astype(BF)
    stream_f = stream.astype(F32)
    mean_square = jnp.mean(stream_f * stream_f, axis=-1, keepdims=True)
    normed = (stream_f * lax.rsqrt(mean_square + 1e-05) * norm_gain).astype(BF)

    other_normed = across(normed)
    shape = (half_count, capacity, width)
    own_rows = exchange(spread(own_send, normed).reshape(shape))
    own_out = expert_ffn(own_rows, w_gate, w_up, w_down)
    other_rows = exchange(spread(other_send, other_normed).reshape(shape))
    other_out = expert_ffn(other_rows, w_gate, w_up, w_down)
    other_back = exchange(other_out).reshape(-1, width)
    other_part = across(gather_back(other_high, other_low, other_back).astype(BF))
    own_back = exchange(own_out).reshape(-1, width)
    mixture = gather_back(own_high, own_low, own_back) + other_part.astype(F32)
    layer_out = (stream_f + mixture).astype(BF)
    return (attended[None], layer_out[None])


def solution(mesh):
    seq_count, exp_count = mesh.shape["seq"], mesh.shape["exp"]
    finer = Mesh(
        mesh.devices.reshape(2, seq_count // 2, exp_count), ("hi", "lo", "exp")
    )
    tokens = P("exp", SEQ)
    experts = P(("hi", "lo", "exp"), None, None)
    return jax.shard_map(
        shards,
        mesh=finer,
        in_specs=(tokens, tokens, P(), tokens, tokens, experts, experts, experts),
        out_specs=(tokens, tokens),
        check_vma=False,
    )
```

```python
import functools
import math

import jax
import jax.numpy as jnp
from jax import lax
from jax.experimental import pallas as pl
from jax.experimental.pallas import tpu as pltpu
from jax.sharding import Mesh
from jax.sharding import PartitionSpec as P


HEADS = 32
SEQ = ("hi", "lo")
HALF = ("lo", "exp")
BF = jnp.bfloat16
F32 = jnp.float32


def attention_kernel(step_rows, qkv_ref, out_ref):
    blocks, _, rows, head_width = qkv_ref.shape
    length = blocks * rows
    factor = math.log2(math.e) / math.sqrt(head_width)
    queries = qkv_ref[:, 0].reshape(length, head_width)
    keys = qkv_ref[:, 1].reshape(length, head_width)
    values = qkv_ref[:, 2].reshape(length, head_width)
    over_width = (((1,), (1,)), ((), ()))
    shape = (step_rows, step_rows)
    seen = lax.broadcasted_iota(jnp.int32, shape, 1) <= lax.broadcasted_iota(jnp.int32, shape, 0)
    for start in range(0, length, step_rows):
        stop = start + step_rows
        part = queries[start:stop]
        near = lax.dot_general(part, keys[start:stop], over_width, preferred_element_type=F32)
        near = jnp.where(seen, near, F32(-1e30))
        highest = jnp.max(near, axis=-1, keepdims=True)
        if start:
            far = lax.dot_general(part, keys[:start], over_width, preferred_element_type=F32)
            highest = jnp.maximum(highest, jnp.max(far, axis=-1, keepdims=True))
        near = jnp.exp2((near - highest) * factor)
        total = jnp.sum(near, axis=-1, keepdims=True)
        mixed = jnp.dot(near.astype(BF), values[start:stop], preferred_element_type=F32)
        if start:
            far = jnp.exp2((far - highest) * factor)
            total += jnp.sum(far, axis=-1, keepdims=True)
            mixed += jnp.dot(far.astype(BF), values[:start], preferred_element_type=F32)
        mixed = (mixed / total).astype(BF)
        for block in range(start // rows, stop // rows):
            low = block * rows - start
            out_ref[block] = mixed[low : low + rows]


def attention(arrived, local_heads):
    blocks, _, rows, local_width = arrived.shape
    head_width = local_width // local_heads
    length = blocks * rows
    return pl.pallas_call(
        functools.partial(attention_kernel, 2 * rows),
        grid=(local_heads,),
        in_specs=[pl.BlockSpec((blocks, 3, rows, head_width), lambda head: (0, 0, 0, head))],
        out_specs=pl.BlockSpec((blocks, rows, head_width), lambda head: (0, 0, head)),
        out_shape=pltpu.HBM((blocks, rows, local_width), BF),
        compiler_params=pltpu.CompilerParams(vmem_limit_bytes=20 << 20),
        cost_estimate=pl.CostEstimate(
            flops=2 * length * length * local_width,
            bytes_accessed=8 * length * local_width,
            transcendentals=length * length * local_heads // 2,
        ),
    )(arrived)


def expert_kernel(rows_ref, gate_hbm, up_hbm, down_hbm, out_ref, gate_ref, up_ref, down_ref, hidden_ref, arrived):
    pieces = arrived.shape[1]
    weights = ((gate_hbm, gate_ref), (up_hbm, up_ref), (down_hbm, down_ref))
    copies = []
    for kind, (source, target) in enumerate(weights):
        depth = target.shape[0] // pieces
        group = []
        for piece in range(pieces):
            part = pl.ds(piece * depth, depth)
            group.append(
                pltpu.make_async_copy(source.at[0, part], target.at[part], arrived.at[kind, piece])
            )
        copies.append(group)
    for copy in copies[0] + copies[1] + copies[2]:
        copy.start()

    def columns_of(width, most):
        tile = math.gcd(width, most)
        return [slice(start, start + tile) for start in range(0, width, tile)]

    rows = rows_ref[...]
    for copy in copies[0]:
        copy.wait()
    gates = []
    for columns in columns_of(gate_ref.shape[1], 256):
        gates.append(jnp.dot(rows, gate_ref[:, columns], preferred_element_type=F32))
    for copy in copies[1]:
        copy.wait()
    for gate, columns in zip(gates, columns_of(gate_ref.shape[1], 256)):
        up = jnp.dot(rows, up_ref[:, columns], preferred_element_type=F32)
        hidden_ref[:, columns] = (gate / (1.0 + jnp.exp(-gate)) * up).astype(BF)
    hidden_rows = hidden_ref[...]
    for copy in copies[2]:
        copy.wait()
    for columns in columns_of(down_ref.shape[1], 512):
        out_ref[:, columns] = jnp.dot(
            hidden_rows, down_ref[:, columns], preferred_element_type=F32
        ).astype(BF)


def in_hbm(array):
    return pltpu.with_memory_space_constraint(array, pltpu.HBM)


def expert_ffn(rows, w_gate, w_up, w_down):
    count, width = rows.shape
    hidden = w_gate.shape[2]
    vmem = pl.BlockSpec(memory_space=pltpu.VMEM)
    hbm = pl.BlockSpec(memory_space=pltpu.HBM)
    return pl.pallas_call(
        expert_kernel,
        in_specs=[vmem, hbm, hbm, hbm],
        out_specs=vmem,
        out_shape=jax.ShapeDtypeStruct((count, width), BF),
        scratch_shapes=[
            pltpu.VMEM((width, hidden), BF),
            pltpu.VMEM((width, hidden), BF),
            pltpu.VMEM((hidden, width), BF),
            pltpu.VMEM((count, hidden), BF),
            pltpu.SemaphoreType.DMA((3, 4)),
        ],
        compiler_params=pltpu.CompilerParams(vmem_limit_bytes=30 << 20),
        cost_estimate=pl.CostEstimate(
            flops=6 * count * width * hidden,
            bytes_accessed=6 * width * hidden + 4 * count * width,
            transcendentals=count * hidden,
        ),
    )(rows, in_hbm(w_gate), in_hbm(w_up), in_hbm(w_down))


def regroup_kernel(in_ref, out_ref, held, arrived, left):
    blocks, _, _, local_width = held.shape
    reads, writes = [], []
    for block in range(blocks):
        columns = pl.ds(block * local_width, local_width)
        reads.append(
            pltpu.make_async_copy(in_ref.at[:, :, columns], held.at[block], arrived.at[block])
        )
        writes.append(pltpu.make_async_copy(held.at[block], out_ref.at[block], left.at[block]))
    for read in reads:
        read.start()
    for read, write in zip(reads, writes):
        read.wait()
        write.start()
    for write in writes:
        write.wait()


def regroup(projected, blocks):
    kinds, rows, width = projected.shape
    shape = (blocks, kinds, rows, width // blocks)
    hbm = pl.BlockSpec(memory_space=pltpu.HBM)
    return pl.pallas_call(
        regroup_kernel,
        in_specs=[hbm],
        out_specs=hbm,
        out_shape=pltpu.HBM(shape, BF),
        scratch_shapes=[
            pltpu.VMEM(shape, BF),
            pltpu.SemaphoreType.DMA((blocks,)),
            pltpu.SemaphoreType.DMA((blocks,)),
        ],
        compiler_params=pltpu.CompilerParams(vmem_limit_bytes=59 << 20),
    )(projected)


def norm_kernel(parts, *refs):
    returned, (patches_ref, gain_ref, attended_ref, stream_ref) = refs[:parts], refs[parts:parts + 4]
    normed_refs = refs[parts + 4 :]
    blocks, _, part_width = returned[0].shape
    total = 0.0
    for block in range(blocks * parts):
        columns = slice(block * part_width, (block + 1) * part_width)
        part = returned[block % parts][block // parts]
        attended_ref[:, columns] = part
        stream = (patches_ref[:, columns].astype(F32) + part.astype(F32)).astype(BF)
        stream_ref[:, columns] = stream
        stream_f = stream.astype(F32)
        total += jnp.sum(stream_f * stream_f, axis=-1, keepdims=True)
    factor = lax.rsqrt(total / (blocks * parts * part_width) + 1e-05)
    start = 0
    for normed_ref in normed_refs:
        stop = start + normed_ref.shape[1]
        stream_f = stream_ref[:, start:stop].astype(F32)
        normed_ref[...] = (stream_f * factor * gain_ref[:, start:stop]).astype(BF)
        start = stop


def residual_norm(returned, patches, gain, chunks):
    blocks, rows, part_width = returned[0].shape
    width = patches.shape[1]
    tile = math.gcd(rows, 32)
    at = lambda step: (step, 0)
    shape = lambda columns: jax.ShapeDtypeStruct((rows, columns), BF)
    return pl.pallas_call(
        functools.partial(norm_kernel, len(returned)),
        grid=(rows // tile,),
        in_specs=[
            pl.BlockSpec((blocks, tile, part_width), lambda step: (0, step, 0)) for _ in returned
        ]
        + [
            pl.BlockSpec((tile, width), at),
            pl.BlockSpec((1, width), lambda step: (0, 0)),
        ],
        out_specs=[pl.BlockSpec((tile, width), at)] * 2
        + [pl.BlockSpec((tile, width // chunks), at)] * chunks,
        out_shape=[pltpu.HBM((rows, width), BF)] * 2 + [shape(width // chunks)] * chunks,
        compiler_params=pltpu.CompilerParams(vmem_limit_bytes=8 << 20),
    )(*returned, patches, gain)


def routing(expert_ids, gate_levels, first, experts, capacity):
    rows = expert_ids.shape[0]
    routed = expert_ids.reshape(-1)
    names = lax.broadcasted_iota(jnp.int32, (2 * rows, 2 * rows), 1)
    same = (routed[:, None] == routed[None, :]) & (
        names < lax.broadcasted_iota(jnp.int32, (2 * rows, 2 * rows), 0)
    )
    slot = jnp.sum(same.astype(jnp.int32), axis=1)
    local = routed - first
    position = jnp.where((local >= 0) & (local < experts), local * capacity + slot, -1)
    position = position.reshape(rows, 2)
    levels = gate_levels.astype(F32)
    share = levels / jnp.sum(levels, axis=-1, keepdims=True)
    places = lax.broadcasted_iota(jnp.int32, (rows, experts * capacity), 1)
    hit0 = places == position[:, 0:1]
    hit1 = places == position[:, 1:2]
    send = (hit0 | hit1).astype(BF)
    weight = jnp.where(hit0, share[:, 0:1], F32(0)) + jnp.where(hit1, share[:, 1:2], F32(0))
    high = lax.reduce_precision(weight, 8, 7)
    return send, high.astype(BF), (weight - high).astype(BF)


def spread(send, rows):
    return lax.dot_general(
        send, rows, (((0,), (0,)), ((), ())), preferred_element_type=F32
    ).astype(BF)


def gather_back(high, low, rows):
    return jnp.dot(high, rows, preferred_element_type=F32) + jnp.dot(
        low, rows, preferred_element_type=F32
    )


def shards(projected, patches, norm_gain, expert_ids, gate_levels, w_gate, w_up, w_down):
    seq_count = lax.axis_size(SEQ)
    half_count = lax.axis_size(HALF)
    lo_count = lax.axis_size("lo")
    tok_rows = patches.shape[1]
    local_heads = HEADS // seq_count
    expert_count = 2 * half_count
    capacity = max(2, 4 * tok_rows // expert_count)
    mirror = [(i, (i + lo_count) % seq_count) for i in range(seq_count)]
    first = lax.axis_index("hi") * half_count

    def across(value):
        return lax.ppermute(value, SEQ, mirror)

    def exchange(axes, value):
        return lax.all_to_all(value, axes, split_axis=0, concat_axis=0, tiled=True)

    def routed(value):
        sent = value.reshape(half_count, capacity, value.shape[1])
        return exchange(HALF, sent).reshape(value.shape)

    other = across(jnp.concatenate([expert_ids[0], gate_levels[0]], axis=1))
    outgoing = regroup(jnp.transpose(projected[0], (1, 0, 2)), seq_count)
    arrived = exchange(SEQ, outgoing)
    arrived, other = lax.optimization_barrier((arrived, other))
    own_send, own_high, own_low = routing(
        expert_ids[0], gate_levels[0], first, half_count, capacity
    )
    other_send, other_high, other_low = routing(
        other[:, :2], other[:, 2:], first, half_count, capacity
    )
    returned = [exchange(SEQ, attention(arrived, local_heads))]
    attended, stream, normed = residual_norm(returned, patches[0], norm_gain[None], 1)

    other_normed = across(normed)
    own_rows = routed(spread(own_send, normed))
    other_rows = routed(spread(other_send, other_normed))
    own_out = expert_ffn(own_rows, w_gate, w_up, w_down)
    other_out = expert_ffn(other_rows, w_gate, w_up, w_down)
    other_back = routed(other_out)
    other_part = across(gather_back(other_high, other_low, other_back).astype(BF))
    own_back = routed(own_out)
    own_total = stream.astype(F32) + gather_back(own_high, own_low, own_back)
    layer_out = (own_total + other_part.astype(F32)).astype(BF)
    return (attended[None], layer_out[None])


def solution(mesh):
    seq_count, exp_count = mesh.shape["seq"], mesh.shape["exp"]
    finer = Mesh(
        mesh.devices.reshape(2, seq_count // 2, exp_count), ("hi", "lo", "exp")
    )
    tokens = P("exp", SEQ)
    experts = P(("hi", "lo", "exp"), None, None)
    return jax.shard_map(
        shards,
        mesh=finer,
        in_specs=(tokens, tokens, P(), tokens, tokens, experts, experts, experts),
        out_specs=(tokens, tokens),
        check_vma=False,
    )
```

```python
import functools
import math

import jax
import jax.numpy as jnp
from jax import lax
from jax.experimental import pallas as pl
from jax.experimental.pallas import tpu as pltpu
from jax.sharding import Mesh
from jax.sharding import PartitionSpec as P


HEADS = 32
SEQ = ("hi", "lo")
HALF = ("lo", "exp")
BF = jnp.bfloat16
F32 = jnp.float32


def attention_kernel(step_rows, qkv_ref, out_ref):
    blocks, _, rows, head_width = qkv_ref.shape
    length = blocks * rows
    factor = math.log2(math.e) / math.sqrt(head_width)
    queries = qkv_ref[:, 0].reshape(length, head_width)
    keys = qkv_ref[:, 1].reshape(length, head_width)
    values = qkv_ref[:, 2].reshape(length, head_width)
    over_width = (((1,), (1,)), ((), ()))
    shape = (step_rows, step_rows)
    seen = lax.broadcasted_iota(jnp.int32, shape, 1) <= lax.broadcasted_iota(jnp.int32, shape, 0)
    for start in range(0, length, step_rows):
        stop = start + step_rows
        part = queries[start:stop]
        near = lax.dot_general(part, keys[start:stop], over_width, preferred_element_type=F32)
        near = jnp.where(seen, near, F32(-1e30))
        highest = jnp.max(near, axis=-1, keepdims=True)
        if start:
            far = lax.dot_general(part, keys[:start], over_width, preferred_element_type=F32)
            highest = jnp.maximum(highest, jnp.max(far, axis=-1, keepdims=True))
        near = jnp.exp2((near - highest) * factor)
        total = jnp.sum(near, axis=-1, keepdims=True)
        mixed = jnp.dot(near.astype(BF), values[start:stop], preferred_element_type=F32)
        if start:
            far = jnp.exp2((far - highest) * factor)
            total += jnp.sum(far, axis=-1, keepdims=True)
            mixed += jnp.dot(far.astype(BF), values[:start], preferred_element_type=F32)
        mixed = (mixed / total).astype(BF)
        for block in range(start // rows, stop // rows):
            low = block * rows - start
            out_ref[block] = mixed[low : low + rows]


def attention(arrived, local_heads):
    blocks, _, rows, local_width = arrived.shape
    head_width = local_width // local_heads
    length = blocks * rows
    return pl.pallas_call(
        functools.partial(attention_kernel, 2 * rows),
        grid=(local_heads,),
        in_specs=[pl.BlockSpec((blocks, 3, rows, head_width), lambda head: (0, 0, 0, head))],
        out_specs=pl.BlockSpec((blocks, rows, head_width), lambda head: (0, 0, head)),
        out_shape=pltpu.HBM((blocks, rows, local_width), BF),
        compiler_params=pltpu.CompilerParams(vmem_limit_bytes=20 << 20),
        cost_estimate=pl.CostEstimate(
            flops=2 * length * length * local_width,
            bytes_accessed=8 * length * local_width,
            transcendentals=length * length * local_heads // 2,
        ),
    )(arrived)


def expert_kernel(rows_ref, gate_hbm, up_hbm, down_hbm, out_hbm, gate_ref, up_ref, down_ref, gate_total, up_total, out_ref, arrived, left):
    pieces = arrived.shape[1]

    def read(kind, source, target, piece):
        depth = target.shape[0] // pieces
        part = pl.ds(piece * depth, depth)
        return pltpu.make_async_copy(source.at[0, part], target.at[part], arrived.at[kind, piece])

    gates = [read(0, gate_hbm, gate_ref, piece) for piece in range(pieces)]
    ups = [read(1, up_hbm, up_ref, piece) for piece in range(pieces)]
    downs = [read(2, down_hbm, down_ref, piece) for piece in range(pieces)]
    for pair in zip(gates, ups):
        for copy in pair:
            copy.start()
    for copy in downs:
        copy.start()

    depth = gate_ref.shape[0] // pieces
    for piece in range(pieces):
        part = slice(piece * depth, (piece + 1) * depth)
        for copy, weight, total in (
            (gates[piece], gate_ref, gate_total),
            (ups[piece], up_ref, up_total),
        ):
            copy.wait()
            term = jnp.dot(rows_ref[:, part], weight[part], preferred_element_type=F32)
            total[...] = total[...] + term if piece else term
    gate = gate_total[...]
    hidden = (gate / (1.0 + jnp.exp(-gate)) * up_total[...]).astype(BF)
    for copy in downs:
        copy.wait()
    width = out_ref.shape[1]
    tile = width // left.shape[0]
    writes = []
    for index in range(left.shape[0]):
        columns = slice(index * tile, (index + 1) * tile)
        out_ref[:, columns] = jnp.dot(
            hidden, down_ref[:, columns], preferred_element_type=F32
        ).astype(BF)
        columns = pl.ds(index * tile, tile)
        write = pltpu.make_async_copy(out_ref.at[:, columns], out_hbm.at[:, columns], left.at[index])
        write.start()
        writes.append(write)
    for write in writes:
        write.wait()


def in_hbm(array):
    return pltpu.with_memory_space_constraint(array, pltpu.HBM)


def expert_ffn(rows, w_gate, w_up, w_down):
    count, width = rows.shape
    hidden = w_gate.shape[2]
    hbm = pl.BlockSpec(memory_space=pltpu.HBM)
    pieces = math.gcd(width // 256, 4)
    return pl.pallas_call(
        expert_kernel,
        in_specs=[pl.BlockSpec(memory_space=pltpu.VMEM), hbm, hbm, hbm],
        out_specs=hbm,
        out_shape=pltpu.HBM((count, width), BF),
        scratch_shapes=[
            pltpu.VMEM((width, hidden), BF),
            pltpu.VMEM((width, hidden), BF),
            pltpu.VMEM((hidden, width), BF),
            pltpu.VMEM((count, hidden), F32),
            pltpu.VMEM((count, hidden), F32),
            pltpu.VMEM((count, width), BF),
            pltpu.SemaphoreType.DMA((3, pieces)),
            pltpu.SemaphoreType.DMA((2 * pieces,)),
        ],
        compiler_params=pltpu.CompilerParams(vmem_limit_bytes=32 << 20),
        cost_estimate=pl.CostEstimate(
            flops=6 * count * width * hidden,
            bytes_accessed=6 * width * hidden + 4 * count * width,
            transcendentals=count * hidden,
        ),
    )(rows, in_hbm(w_gate), in_hbm(w_up), in_hbm(w_down))


def regroup_kernel(in_ref, out_ref, held, arrived, left):
    blocks, _, _, local_width = held.shape
    reads, writes = [], []
    for block in range(blocks):
        columns = pl.ds(block * local_width, local_width)
        reads.append(
            pltpu.make_async_copy(in_ref.at[:, :, columns], held.at[block], arrived.at[block])
        )
        writes.append(pltpu.make_async_copy(held.at[block], out_ref.at[block], left.at[block]))
    for read in reads:
        read.start()
    for read, write in zip(reads, writes):
        read.wait()
        write.start()
    for write in writes:
        write.wait()


def regroup(projected, blocks):
    kinds, rows, width = projected.shape
    shape = (blocks, kinds, rows, width // blocks)
    hbm = pl.BlockSpec(memory_space=pltpu.HBM)
    return pl.pallas_call(
        regroup_kernel,
        in_specs=[hbm],
        out_specs=hbm,
        out_shape=pltpu.HBM(shape, BF),
        scratch_shapes=[
            pltpu.VMEM(shape, BF),
            pltpu.SemaphoreType.DMA((blocks,)),
            pltpu.SemaphoreType.DMA((blocks,)),
        ],
        compiler_params=pltpu.CompilerParams(vmem_limit_bytes=59 << 20),
    )(projected)


def norm_kernel(parts, *refs):
    returned, (patches_ref, gain_ref, attended_ref, stream_ref) = refs[:parts], refs[parts:parts + 4]
    normed_refs = refs[parts + 4 :]
    blocks, _, part_width = returned[0].shape
    total = 0.0
    for block in range(blocks * parts):
        columns = slice(block * part_width, (block + 1) * part_width)
        part = returned[block % parts][block // parts]
        attended_ref[:, columns] = part
        stream = (patches_ref[:, columns].astype(F32) + part.astype(F32)).astype(BF)
        stream_ref[:, columns] = stream
        stream_f = stream.astype(F32)
        total += jnp.sum(stream_f * stream_f, axis=-1, keepdims=True)
    factor = lax.rsqrt(total / (blocks * parts * part_width) + 1e-05)
    start = 0
    for normed_ref in normed_refs:
        stop = start + normed_ref.shape[1]
        stream_f = stream_ref[:, start:stop].astype(F32)
        normed_ref[...] = (stream_f * factor * gain_ref[:, start:stop]).astype(BF)
        start = stop


def residual_norm(returned, patches, gain, chunks):
    blocks, rows, part_width = returned[0].shape
    width = patches.shape[1]
    tile = math.gcd(rows, 32)
    at = lambda step: (step, 0)
    shape = lambda columns: jax.ShapeDtypeStruct((rows, columns), BF)
    return pl.pallas_call(
        functools.partial(norm_kernel, len(returned)),
        grid=(rows // tile,),
        in_specs=[
            pl.BlockSpec((blocks, tile, part_width), lambda step: (0, step, 0)) for _ in returned
        ]
        + [
            pl.BlockSpec((tile, width), at),
            pl.BlockSpec((1, width), lambda step: (0, 0)),
        ],
        out_specs=[pl.BlockSpec((tile, width), at)] * 2
        + [pl.BlockSpec((tile, width // chunks), at)] * chunks,
        out_shape=[pltpu.HBM((rows, width), BF)] * 2 + [shape(width // chunks)] * chunks,
        compiler_params=pltpu.CompilerParams(vmem_limit_bytes=8 << 20),
    )(*returned, patches, gain)


def routing(expert_ids, gate_levels, first, experts, capacity):
    rows = expert_ids.shape[0]
    routed = expert_ids.reshape(-1)
    names = lax.broadcasted_iota(jnp.int32, (2 * rows, 2 * rows), 1)
    same = (routed[:, None] == routed[None, :]) & (
        names < lax.broadcasted_iota(jnp.int32, (2 * rows, 2 * rows), 0)
    )
    slot = jnp.sum(same.astype(jnp.int32), axis=1)
    local = routed - first
    position = jnp.where((local >= 0) & (local < experts), local * capacity + slot, -1)
    position = position.reshape(rows, 2)
    levels = gate_levels.astype(F32)
    share = levels / jnp.sum(levels, axis=-1, keepdims=True)
    places = lax.broadcasted_iota(jnp.int32, (rows, experts * capacity), 1)
    hit0 = places == position[:, 0:1]
    hit1 = places == position[:, 1:2]
    send = (hit0 | hit1).astype(BF)
    weight = jnp.where(hit0, share[:, 0:1], F32(0)) + jnp.where(hit1, share[:, 1:2], F32(0))
    high = lax.reduce_precision(weight, 8, 7)
    return send, high.astype(BF), (weight - high).astype(BF)


def spread(send, rows):
    return lax.dot_general(
        send, rows, (((0,), (0,)), ((), ())), preferred_element_type=F32
    ).astype(BF)


def gather_back(high, low, rows):
    return jnp.dot(high, rows, preferred_element_type=F32) + jnp.dot(
        low, rows, preferred_element_type=F32
    )


def finish_kernel(high_ref, low_ref, back_ref, stream_ref, other_ref, out_ref):
    mixture = gather_back(high_ref[...], low_ref[...], back_ref[...])
    total = stream_ref[...].astype(F32) + (mixture + other_ref[...].astype(F32))
    out_ref[...] = total.astype(BF)


def finish(high, low, back, stream, other):
    rows, width = stream.shape
    tile = math.gcd(width, 1024)
    weight = pl.BlockSpec(high.shape, lambda step: (0, 0))
    columns = pl.BlockSpec((rows, tile), lambda step: (0, step))
    return pl.pallas_call(
        finish_kernel,
        grid=(width // tile,),
        in_specs=[
            weight,
            weight,
            pl.BlockSpec((back.shape[0], tile), lambda step: (0, step)),
            columns,
            columns,
        ],
        out_specs=columns,
        out_shape=pltpu.HBM((rows, width), BF),
        compiler_params=pltpu.CompilerParams(vmem_limit_bytes=16 << 20),
    )(high, low, back, stream, other)


def shards(projected, patches, norm_gain, expert_ids, gate_levels, w_gate, w_up, w_down):
    seq_count = lax.axis_size(SEQ)
    half_count = lax.axis_size(HALF)
    lo_count = lax.axis_size("lo")
    tok_rows = patches.shape[1]
    local_heads = HEADS // seq_count
    expert_count = 2 * half_count
    capacity = max(2, 4 * tok_rows // expert_count)
    turned = [(i + lo_count // 2) % lo_count for i in range(lo_count)]
    mirror = [
        (i, (1 - i // lo_count) * lo_count + turned[i % lo_count]) for i in range(seq_count)
    ]
    first = lax.axis_index("hi") * half_count

    def across(value):
        return lax.ppermute(value, SEQ, mirror)

    def exchange(axes, value):
        return lax.all_to_all(value, axes, split_axis=0, concat_axis=0, tiled=True)

    def routed(value):
        sent = value.reshape(half_count, capacity, value.shape[1])
        return exchange(HALF, sent).reshape(value.shape)

    other = across(jnp.concatenate([expert_ids[0], gate_levels[0]], axis=1))
    outgoing = regroup(jnp.transpose(projected[0], (1, 0, 2)), seq_count)
    arrived = exchange(SEQ, outgoing)
    own_send, own_high, own_low = routing(
        expert_ids[0], gate_levels[0], first, half_count, capacity
    )
    other_send, other_high, other_low = routing(
        other[:, :2], other[:, 2:], first, half_count, capacity
    )
    arrived, own_send, own_high, own_low, other_send, other_high, other_low = (
        lax.optimization_barrier(
            (arrived, own_send, own_high, own_low, other_send, other_high, other_low)
        )
    )
    returned = [exchange(SEQ, attention(arrived, local_heads))]
    attended, stream, normed = residual_norm(returned, patches[0], norm_gain[None], 1)

    other_normed = across(normed)
    own_rows = routed(spread(own_send, normed))
    other_rows = routed(spread(other_send, other_normed))
    own_out = expert_ffn(own_rows, w_gate, w_up, w_down)
    other_out = expert_ffn(other_rows, w_gate, w_up, w_down)
    other_back = routed(other_out)
    other_part = across(gather_back(other_high, other_low, other_back).astype(BF))
    own_back = routed(own_out)
    layer_out = finish(own_high, own_low, own_back, stream, other_part)
    return (attended[None], layer_out[None])


def solution(mesh):
    seq_count, exp_count = mesh.shape["seq"], mesh.shape["exp"]
    finer = Mesh(
        mesh.devices.reshape(2, seq_count // 2, exp_count), ("hi", "lo", "exp")
    )
    tokens = P("exp", SEQ)
    experts = P(("hi", "lo", "exp"), None, None)
    return jax.shard_map(
        shards,
        mesh=finer,
        in_specs=(tokens, tokens, P(), tokens, tokens, experts, experts, experts),
        out_specs=(tokens, tokens),
        check_vma=False,
    )
```

```python
import functools
import math

import jax
import jax.numpy as jnp
from jax import lax
from jax.experimental import pallas as pl
from jax.experimental.pallas import tpu as pltpu
from jax.sharding import Mesh
from jax.sharding import PartitionSpec as P


HEADS = 32
SEQ = ("hi", "lo")
HALF = ("lo", "exp")
BF = jnp.bfloat16
F32 = jnp.float32


def attention_kernel(step_rows, qkv_ref, out_ref):
    blocks, _, rows, head_width = qkv_ref.shape
    length = blocks * rows
    factor = math.log2(math.e) / math.sqrt(head_width)
    queries = qkv_ref[:, 0].reshape(length, head_width)
    keys = qkv_ref[:, 1].reshape(length, head_width)
    values = qkv_ref[:, 2].reshape(length, head_width).T
    over_width = (((1,), (1,)), ((), ()))
    shape = (step_rows, step_rows)
    seen = lax.broadcasted_iota(jnp.int32, shape, 0) <= lax.broadcasted_iota(jnp.int32, shape, 1)
    half = step_rows // 2
    starts = range(0, length, step_rows)
    scores = []
    for start in starts:
        middle, stop = start + half, start + step_rows
        part = queries[start:stop]
        pieces = [
            lax.dot_general(keys[start:middle], part, over_width, preferred_element_type=F32),
            lax.dot_general(
                keys[middle:stop], part[half:], over_width, preferred_element_type=F32
            ),
        ]
        pieces[0] = jnp.where(seen[:half], pieces[0], F32(-1e30))
        pieces[1] = jnp.where(seen[:half, :half], pieces[1], F32(-1e30))
        if start:
            pieces.append(
                lax.dot_general(keys[:start], part, over_width, preferred_element_type=F32)
            )
        scores.append(pieces)
    for start, (near, last, *far) in zip(starts, scores):
        middle, stop = start + half, start + step_rows
        highest = jnp.max(near, axis=0, keepdims=True)
        for piece in far:
            highest = jnp.maximum(highest, jnp.max(piece, axis=0, keepdims=True))
        high_last = jnp.maximum(highest[:, half:], jnp.max(last, axis=0, keepdims=True))
        highest = jnp.concatenate([highest[:, :half], high_last], axis=1)
        near = jnp.exp2((near - highest) * factor)
        total = jnp.sum(near, axis=0, keepdims=True)
        mixed = jnp.dot(values[:, start:middle], near.astype(BF), preferred_element_type=F32)
        for piece in far:
            piece = jnp.exp2((piece - highest) * factor)
            total += jnp.sum(piece, axis=0, keepdims=True)
            mixed += jnp.dot(values[:, :start], piece.astype(BF), preferred_element_type=F32)
        last = jnp.exp2((last - high_last) * factor)
        total_last = total[:, half:] + jnp.sum(last, axis=0, keepdims=True)
        mixed_last = mixed[:, half:] + jnp.dot(
            values[:, middle:stop], last.astype(BF), preferred_element_type=F32
        )
        mixed = jnp.concatenate(
            [mixed[:, :half] / total[:, :half], mixed_last / total_last], axis=1
        )
        mixed = mixed.T.astype(BF)
        for block in range(start // rows, stop // rows):
            low = block * rows - start
            out_ref[block] = mixed[low : low + rows]


def attention(arrived, local_heads):
    blocks, _, rows, local_width = arrived.shape
    head_width = local_width // local_heads
    length = blocks * rows
    return pl.pallas_call(
        functools.partial(attention_kernel, 4 * rows),
        grid=(local_heads,),
        in_specs=[pl.BlockSpec((blocks, 3, rows, head_width), lambda head: (0, 0, 0, head))],
        out_specs=pl.BlockSpec((blocks, rows, head_width), lambda head: (0, 0, head)),
        out_shape=pltpu.HBM((blocks, rows, local_width), BF),
        compiler_params=pltpu.CompilerParams(vmem_limit_bytes=20 << 20),
        cost_estimate=pl.CostEstimate(
            flops=2 * length * length * local_width,
            bytes_accessed=8 * length * local_width,
            transcendentals=length * length * local_heads // 2,
        ),
    )(arrived)


def expert_kernel(rows_hbm, gate_hbm, up_hbm, down_hbm, out_hbm, rows_ref, gate_ref, up_ref, down_ref, gate_total, up_total, out_ref, arrived, left):
    pieces = arrived.shape[1]

    def read(kind, source, target, piece):
        depth = target.shape[0] // pieces
        part = pl.ds(piece * depth, depth)
        return pltpu.make_async_copy(source.at[0, part], target.at[part], arrived.at[kind, piece])

    gates = [read(0, gate_hbm, gate_ref, piece) for piece in range(pieces)]
    ups = [read(1, up_hbm, up_ref, piece) for piece in range(pieces)]
    downs = [read(2, down_hbm, down_ref, piece) for piece in range(pieces)]
    depth = gate_ref.shape[0] // pieces
    rows = []
    for piece in range(pieces):
        part = pl.ds(piece * depth, depth)
        rows.append(
            pltpu.make_async_copy(
                rows_hbm.at[:, part], rows_ref.at[:, part], arrived.at[3, piece]
            )
        )
    for group in zip(rows, gates, ups):
        for copy in group:
            copy.start()
    for copy in downs:
        copy.start()

    for piece in range(pieces):
        part = slice(piece * depth, (piece + 1) * depth)
        rows[piece].wait()
        for copy, weight, total in (
            (gates[piece], gate_ref, gate_total),
            (ups[piece], up_ref, up_total),
        ):
            copy.wait()
            term = jnp.dot(rows_ref[:, part], weight[part], preferred_element_type=F32)
            total[...] = total[...] + term if piece else term
    gate = gate_total[...]
    hidden = (gate / (1.0 + jnp.exp(-gate)) * up_total[...]).astype(BF)
    for copy in downs:
        copy.wait()
    width = out_ref.shape[1]
    tile = width // left.shape[0]
    writes = []
    for index in range(left.shape[0]):
        columns = slice(index * tile, (index + 1) * tile)
        out_ref[:, columns] = jnp.dot(
            hidden, down_ref[:, columns], preferred_element_type=F32
        ).astype(BF)
        columns = pl.ds(index * tile, tile)
        write = pltpu.make_async_copy(out_ref.at[:, columns], out_hbm.at[:, columns], left.at[index])
        write.start()
        writes.append(write)
    for write in writes:
        write.wait()


def in_hbm(array):
    return pltpu.with_memory_space_constraint(array, pltpu.HBM)


def expert_ffn(rows, w_gate, w_up, w_down):
    count, width = rows.shape
    hidden = w_gate.shape[2]
    hbm = pl.BlockSpec(memory_space=pltpu.HBM)
    pieces = math.gcd(width // 256, 4)
    return pl.pallas_call(
        expert_kernel,
        in_specs=[pl.BlockSpec(memory_space=pl.ANY), hbm, hbm, hbm],
        out_specs=hbm,
        out_shape=pltpu.HBM((count, width), BF),
        scratch_shapes=[
            pltpu.VMEM((count, width), BF),
            pltpu.VMEM((width, hidden), BF),
            pltpu.VMEM((width, hidden), BF),
            pltpu.VMEM((hidden, width), BF),
            pltpu.VMEM((count, hidden), F32),
            pltpu.VMEM((count, hidden), F32),
            pltpu.VMEM((count, width), BF),
            pltpu.SemaphoreType.DMA((4, pieces)),
            pltpu.SemaphoreType.DMA((2 * pieces,)),
        ],
        compiler_params=pltpu.CompilerParams(vmem_limit_bytes=32 << 20),
        cost_estimate=pl.CostEstimate(
            flops=6 * count * width * hidden,
            bytes_accessed=6 * width * hidden + 4 * count * width,
            transcendentals=count * hidden,
        ),
    )(rows, in_hbm(w_gate), in_hbm(w_up), in_hbm(w_down))


def regroup_kernel(in_ref, out_ref, held, arrived, left):
    blocks, _, _, local_width = held.shape
    reads, writes = [], []
    for block in range(blocks):
        columns = pl.ds(block * local_width, local_width)
        reads.append(
            pltpu.make_async_copy(in_ref.at[:, :, columns], held.at[block], arrived.at[block])
        )
        writes.append(pltpu.make_async_copy(held.at[block], out_ref.at[block], left.at[block]))
    for read in reads:
        read.start()
    for read, write in zip(reads, writes):
        read.wait()
        write.start()
    for write in writes:
        write.wait()


def regroup(projected, blocks):
    kinds, rows, width = projected.shape
    shape = (blocks, kinds, rows, width // blocks)
    hbm = pl.BlockSpec(memory_space=pltpu.HBM)
    return pl.pallas_call(
        regroup_kernel,
        in_specs=[hbm],
        out_specs=hbm,
        out_shape=pltpu.HBM(shape, BF),
        scratch_shapes=[
            pltpu.VMEM(shape, BF),
            pltpu.SemaphoreType.DMA((blocks,)),
            pltpu.SemaphoreType.DMA((blocks,)),
        ],
        compiler_params=pltpu.CompilerParams(vmem_limit_bytes=59 << 20),
    )(projected)


def norm_kernel(parts, *refs):
    returned, (patches_ref, gain_ref, attended_ref, stream_ref) = refs[:parts], refs[parts:parts + 4]
    normed_refs = refs[parts + 4 :]
    blocks, _, part_width = returned[0].shape
    total = 0.0
    for block in range(blocks * parts):
        columns = slice(block * part_width, (block + 1) * part_width)
        part = returned[block % parts][block // parts]
        attended_ref[:, columns] = part
        stream = (patches_ref[:, columns].astype(F32) + part.astype(F32)).astype(BF)
        stream_ref[:, columns] = stream
        stream_f = stream.astype(F32)
        total += jnp.sum(stream_f * stream_f, axis=-1, keepdims=True)
    factor = lax.rsqrt(total / (blocks * parts * part_width) + 1e-05)
    start = 0
    for normed_ref in normed_refs:
        stop = start + normed_ref.shape[1]
        stream_f = stream_ref[:, start:stop].astype(F32)
        normed_ref[...] = (stream_f * factor * gain_ref[:, start:stop]).astype(BF)
        start = stop


def residual_norm(returned, patches, gain, chunks):
    blocks, rows, part_width = returned[0].shape
    width = patches.shape[1]
    tile = math.gcd(rows, 32)
    at = lambda step: (step, 0)
    shape = lambda columns: jax.ShapeDtypeStruct((rows, columns), BF)
    return pl.pallas_call(
        functools.partial(norm_kernel, len(returned)),
        grid=(rows // tile,),
        in_specs=[
            pl.BlockSpec((blocks, tile, part_width), lambda step: (0, step, 0)) for _ in returned
        ]
        + [
            pl.BlockSpec((tile, width), at),
            pl.BlockSpec((1, width), lambda step: (0, 0)),
        ],
        out_specs=[pl.BlockSpec((tile, width), at)] * 2
        + [pl.BlockSpec((tile, width // chunks), at)] * chunks,
        out_shape=[pltpu.HBM((rows, width), BF)] * 2 + [shape(width // chunks)] * chunks,
        compiler_params=pltpu.CompilerParams(vmem_limit_bytes=8 << 20),
    )(*returned, patches, gain)


def routing(expert_ids, gate_levels, first, experts, capacity):
    rows = expert_ids.shape[0]
    routed = expert_ids.reshape(-1)
    names = lax.broadcasted_iota(jnp.int32, (2 * rows, 2 * rows), 1)
    same = (routed[:, None] == routed[None, :]) & (
        names < lax.broadcasted_iota(jnp.int32, (2 * rows, 2 * rows), 0)
    )
    slot = jnp.sum(same.astype(jnp.int32), axis=1)
    local = routed - first
    position = jnp.where((local >= 0) & (local < experts), local * capacity + slot, -1)
    position = position.reshape(rows, 2)
    levels = gate_levels.astype(F32)
    share = levels / jnp.sum(levels, axis=-1, keepdims=True)
    places = lax.broadcasted_iota(jnp.int32, (rows, experts * capacity), 1)
    hit0 = places == position[:, 0:1]
    hit1 = places == position[:, 1:2]
    send = (hit0 | hit1).astype(BF)
    weight = jnp.where(hit0, share[:, 0:1], F32(0)) + jnp.where(hit1, share[:, 1:2], F32(0))
    high = lax.reduce_precision(weight, 8, 7)
    return send, high.astype(BF), (weight - high).astype(BF)


def spread(send, rows):
    return lax.dot_general(
        send, rows, (((0,), (0,)), ((), ())), preferred_element_type=F32
    ).astype(BF)


def gather_back(high, low, rows):
    return jnp.dot(high, rows, preferred_element_type=F32) + jnp.dot(
        low, rows, preferred_element_type=F32
    )


def finish_kernel(high_ref, low_ref, back_ref, stream_ref, other_ref, out_hbm, out_ref, left):
    tile = out_ref.shape[1] // left.shape[0]
    writes = []
    for index in range(left.shape[0]):
        columns = slice(index * tile, (index + 1) * tile)
        mixture = gather_back(high_ref[...], low_ref[...], back_ref[:, columns])
        mixture = mixture + other_ref[:, columns].astype(F32)
        out_ref[:, columns] = (stream_ref[:, columns].astype(F32) + mixture).astype(BF)
        columns = pl.ds(index * tile, tile)
        write = pltpu.make_async_copy(out_ref.at[:, columns], out_hbm.at[:, columns], left.at[index])
        write.start()
        writes.append(write)
    for write in writes:
        write.wait()


def finish(high, low, back, stream, other):
    rows, width = stream.shape
    vmem = pl.BlockSpec(memory_space=pltpu.VMEM)
    return pl.pallas_call(
        finish_kernel,
        in_specs=[vmem] * 5,
        out_specs=pl.BlockSpec(memory_space=pltpu.HBM),
        out_shape=pltpu.HBM((rows, width), BF),
        scratch_shapes=[
            pltpu.VMEM((rows, width), BF),
            pltpu.SemaphoreType.DMA((math.gcd(width // 256, 4),)),
        ],
        compiler_params=pltpu.CompilerParams(vmem_limit_bytes=16 << 20),
    )(high, low, back, stream, other)


def shards(projected, patches, norm_gain, expert_ids, gate_levels, w_gate, w_up, w_down):
    seq_count = lax.axis_size(SEQ)
    half_count = lax.axis_size(HALF)
    lo_count = lax.axis_size("lo")
    tok_rows = patches.shape[1]
    local_heads = HEADS // seq_count
    expert_count = 2 * half_count
    capacity = max(2, 4 * tok_rows // expert_count)
    turned = [(i + lo_count // 2) % lo_count for i in range(lo_count)]
    mirror = [
        (i, (1 - i // lo_count) * lo_count + turned[i % lo_count]) for i in range(seq_count)
    ]
    first = lax.axis_index("hi") * half_count

    def across(value):
        return lax.ppermute(value, SEQ, mirror)

    def exchange(axes, value):
        return lax.all_to_all(value, axes, split_axis=0, concat_axis=0, tiled=True)

    def routed(value):
        sent = value.reshape(half_count, capacity, value.shape[1])
        return exchange(HALF, sent).reshape(value.shape)

    other = across(jnp.concatenate([expert_ids[0], gate_levels[0]], axis=1))
    outgoing = regroup(jnp.transpose(projected[0], (1, 0, 2)), seq_count)
    arrived = exchange(SEQ, outgoing)
    own_send, own_high, own_low = routing(
        expert_ids[0], gate_levels[0], first, half_count, capacity
    )
    other_send, other_high, other_low = routing(
        other[:, :2], other[:, 2:], first, half_count, capacity
    )
    arrived, own_send, own_high, own_low, other_send, other_high, other_low = (
        lax.optimization_barrier(
            (arrived, own_send, own_high, own_low, other_send, other_high, other_low)
        )
    )
    returned = [exchange(SEQ, attention(arrived, local_heads))]
    attended, stream, normed = residual_norm(returned, patches[0], norm_gain[None], 1)

    other_normed = across(normed)
    own_rows = routed(spread(own_send, normed))
    other_rows = routed(spread(other_send, other_normed))
    own_out = expert_ffn(own_rows, w_gate, w_up, w_down)
    other_out = expert_ffn(other_rows, w_gate, w_up, w_down)
    other_back = routed(other_out)
    other_part = across(gather_back(other_high, other_low, other_back).astype(BF))
    own_back = routed(own_out)
    layer_out = finish(own_high, own_low, own_back, stream, other_part)
    return (attended[None], layer_out[None])


def solution(mesh):
    seq_count, exp_count = mesh.shape["seq"], mesh.shape["exp"]
    finer = Mesh(
        mesh.devices.reshape(2, seq_count // 2, exp_count), ("hi", "lo", "exp")
    )
    tokens = P("exp", SEQ)
    experts = P(("hi", "lo", "exp"), None, None)
    return jax.shard_map(
        shards,
        mesh=finer,
        in_specs=(tokens, tokens, P(), tokens, tokens, experts, experts, experts),
        out_specs=(tokens, tokens),
        check_vma=False,
    )
```

```python
import functools
import math

import jax
import jax.numpy as jnp
from jax import lax
from jax.experimental import pallas as pl
from jax.experimental.pallas import tpu as pltpu
from jax.sharding import Mesh
from jax.sharding import PartitionSpec as P


HEADS = 32
SEQ = ("hi", "lo")
HALF = ("lo", "exp")
BF = jnp.bfloat16
F32 = jnp.float32


def turns(count):
    return [*range(count - 2, 0, -1), count - 1]


def attention_kernel(step_rows, me_ref, *refs):
    *refs, qkv_ref, mixed_ref = refs
    blocks, _, rows, head_width = qkv_ref.shape
    pieces, out_refs = refs[:blocks], refs[blocks:]
    for turn, piece in enumerate(pieces):
        qkv_ref[jnp.bitwise_xor(me_ref[0], turn)] = piece[...]
    length = blocks * rows
    factor = math.log2(math.e) / math.sqrt(head_width)
    queries = qkv_ref[:, 0].reshape(length, head_width)
    keys = qkv_ref[:, 1].reshape(length, head_width)
    values = qkv_ref[:, 2].reshape(length, head_width).T
    over_width = (((1,), (1,)), ((), ()))
    shape = (step_rows, step_rows)
    seen = lax.broadcasted_iota(jnp.int32, shape, 0) <= lax.broadcasted_iota(jnp.int32, shape, 1)
    half = step_rows // 2
    starts = range(0, length, step_rows)
    scores = []
    for start in starts:
        middle, stop = start + half, start + step_rows
        part = queries[start:stop]
        pieces = [
            lax.dot_general(keys[start:middle], part, over_width, preferred_element_type=F32),
            lax.dot_general(
                keys[middle:stop], part[half:], over_width, preferred_element_type=F32
            ),
        ]
        pieces[0] = jnp.where(seen[:half], pieces[0], F32(-1e30))
        pieces[1] = jnp.where(seen[:half, :half], pieces[1], F32(-1e30))
        if start:
            pieces.append(
                lax.dot_general(keys[:start], part, over_width, preferred_element_type=F32)
            )
        scores.append(pieces)
    for start, (near, last, *far) in zip(starts, scores):
        middle, stop = start + half, start + step_rows
        highest = jnp.max(near, axis=0, keepdims=True)
        for piece in far:
            highest = jnp.maximum(highest, jnp.max(piece, axis=0, keepdims=True))
        high_last = jnp.maximum(highest[:, half:], jnp.max(last, axis=0, keepdims=True))
        highest = jnp.concatenate([highest[:, :half], high_last], axis=1)
        near = jnp.exp2((near - highest) * factor)
        total = jnp.sum(near, axis=0, keepdims=True)
        mixed = jnp.dot(values[:, start:middle], near.astype(BF), preferred_element_type=F32)
        for piece in far:
            piece = jnp.exp2((piece - highest) * factor)
            total += jnp.sum(piece, axis=0, keepdims=True)
            mixed += jnp.dot(values[:, :start], piece.astype(BF), preferred_element_type=F32)
        last = jnp.exp2((last - high_last) * factor)
        total_last = total[:, half:] + jnp.sum(last, axis=0, keepdims=True)
        mixed_last = mixed[:, half:] + jnp.dot(
            values[:, middle:stop], last.astype(BF), preferred_element_type=F32
        )
        mixed = jnp.concatenate(
            [mixed[:, :half] / total[:, :half], mixed_last / total_last], axis=1
        )
        mixed = mixed.T.astype(BF)
        for block in range(start // rows, stop // rows):
            low = block * rows - start
            mixed_ref[block] = mixed[low : low + rows]
    for turn, out_ref in enumerate(out_refs):
        out_ref[...] = mixed_ref[jnp.bitwise_xor(me_ref[0], turn)]


def attention(me, pieces, local_heads):
    blocks = len(pieces)
    _, rows, local_width = pieces[0].shape
    head_width = local_width // local_heads
    length = blocks * rows
    piece = pl.BlockSpec((3, rows, head_width), lambda head: (0, 0, head))
    return pl.pallas_call(
        functools.partial(attention_kernel, 4 * rows),
        grid=(local_heads,),
        in_specs=[pl.BlockSpec(memory_space=pltpu.SMEM)] + [piece] * blocks,
        out_specs=[pl.BlockSpec((rows, head_width), lambda head: (0, head))] * blocks,
        out_shape=[pltpu.HBM((rows, local_width), BF)] * blocks,
        scratch_shapes=[
            pltpu.VMEM((blocks, 3, rows, head_width), BF),
            pltpu.VMEM((blocks, rows, head_width), BF),
        ],
        compiler_params=pltpu.CompilerParams(vmem_limit_bytes=20 << 20),
        cost_estimate=pl.CostEstimate(
            flops=2 * length * length * local_width,
            bytes_accessed=8 * length * local_width,
            transcendentals=length * length * local_heads // 2,
        ),
    )(me, *pieces)


def expert_kernel(rows_hbm, gate_hbm, up_hbm, down_hbm, out_hbm, rows_ref, gate_ref, up_ref, down_ref, gate_total, up_total, out_ref, arrived, left):
    pieces = arrived.shape[1]

    def read(kind, source, target, piece):
        depth = target.shape[0] // pieces
        part = pl.ds(piece * depth, depth)
        return pltpu.make_async_copy(source.at[0, part], target.at[part], arrived.at[kind, piece])

    gates = [read(0, gate_hbm, gate_ref, piece) for piece in range(pieces)]
    ups = [read(1, up_hbm, up_ref, piece) for piece in range(pieces)]
    downs = [read(2, down_hbm, down_ref, piece) for piece in range(pieces)]
    depth = gate_ref.shape[0] // pieces
    rows = []
    for piece in range(pieces):
        part = pl.ds(piece * depth, depth)
        rows.append(
            pltpu.make_async_copy(
                rows_hbm.at[:, part], rows_ref.at[:, part], arrived.at[3, piece]
            )
        )
    for group in zip(rows, gates, ups):
        for copy in group:
            copy.start()
    for copy in downs:
        copy.start()

    for piece in range(pieces):
        part = slice(piece * depth, (piece + 1) * depth)
        rows[piece].wait()
        for copy, weight, total in (
            (gates[piece], gate_ref, gate_total),
            (ups[piece], up_ref, up_total),
        ):
            copy.wait()
            term = jnp.dot(rows_ref[:, part], weight[part], preferred_element_type=F32)
            total[...] = total[...] + term if piece else term
    gate = gate_total[...]
    hidden = (gate / (1.0 + jnp.exp(-gate)) * up_total[...]).astype(BF)
    for copy in downs:
        copy.wait()
    width = out_ref.shape[1]
    tile = width // left.shape[0]
    writes = []
    for index in range(left.shape[0]):
        columns = slice(index * tile, (index + 1) * tile)
        out_ref[:, columns] = jnp.dot(
            hidden, down_ref[:, columns], preferred_element_type=F32
        ).astype(BF)
        columns = pl.ds(index * tile, tile)
        write = pltpu.make_async_copy(out_ref.at[:, columns], out_hbm.at[:, columns], left.at[index])
        write.start()
        writes.append(write)
    for write in writes:
        write.wait()


def in_hbm(array):
    return pltpu.with_memory_space_constraint(array, pltpu.HBM)


def expert_ffn(rows, w_gate, w_up, w_down):
    count, width = rows.shape
    hidden = w_gate.shape[2]
    hbm = pl.BlockSpec(memory_space=pltpu.HBM)
    pieces = math.gcd(width // 256, 4)
    return pl.pallas_call(
        expert_kernel,
        in_specs=[pl.BlockSpec(memory_space=pl.ANY), hbm, hbm, hbm],
        out_specs=hbm,
        out_shape=pltpu.HBM((count, width), BF),
        scratch_shapes=[
            pltpu.VMEM((count, width), BF),
            pltpu.VMEM((width, hidden), BF),
            pltpu.VMEM((width, hidden), BF),
            pltpu.VMEM((hidden, width), BF),
            pltpu.VMEM((count, hidden), F32),
            pltpu.VMEM((count, hidden), F32),
            pltpu.VMEM((count, width), BF),
            pltpu.SemaphoreType.DMA((4, pieces)),
            pltpu.SemaphoreType.DMA((2 * pieces,)),
        ],
        compiler_params=pltpu.CompilerParams(vmem_limit_bytes=32 << 20),
        cost_estimate=pl.CostEstimate(
            flops=6 * count * width * hidden,
            bytes_accessed=6 * width * hidden + 4 * count * width,
            transcendentals=count * hidden,
        ),
    )(rows, in_hbm(w_gate), in_hbm(w_up), in_hbm(w_down))


def regroup_kernel(me_ref, in_ref, *refs):
    *out_refs, held, arrived, left = refs
    _, _, _, local_width = held.shape
    reads, writes = [], []
    for turn, out_ref in enumerate(out_refs):
        block = jnp.bitwise_xor(me_ref[0], turn)
        columns = pl.ds(pl.multiple_of(block * local_width, local_width), local_width)
        reads.append(
            pltpu.make_async_copy(in_ref.at[:, :, columns], held.at[turn], arrived.at[turn])
        )
        writes.append(pltpu.make_async_copy(held.at[turn], out_ref, left.at[turn]))
    for read in reads:
        read.start()
    for read, write in zip(reads, writes):
        read.wait()
        write.start()
    for write in writes:
        write.wait()


def regroup(me, projected, blocks):
    kinds, rows, width = projected.shape
    shape = (kinds, rows, width // blocks)
    hbm = pl.BlockSpec(memory_space=pltpu.HBM)
    return pl.pallas_call(
        regroup_kernel,
        in_specs=[pl.BlockSpec(memory_space=pltpu.SMEM), hbm],
        out_specs=[hbm] * blocks,
        out_shape=[pltpu.HBM(shape, BF)] * blocks,
        scratch_shapes=[
            pltpu.VMEM((blocks,) + shape, BF),
            pltpu.SemaphoreType.DMA((blocks,)),
            pltpu.SemaphoreType.DMA((blocks,)),
        ],
        compiler_params=pltpu.CompilerParams(vmem_limit_bytes=59 << 20),
    )(me, projected)


def norm_kernel(me_ref, *refs):
    *pieces, patches_ref, gain_ref, attended_ref, stream_ref, normed_ref = refs
    part_width = pieces[0].shape[1]
    total = 0.0
    for turn, piece in enumerate(pieces):
        block = jnp.bitwise_xor(me_ref[0], turn)
        columns = pl.ds(pl.multiple_of(block * part_width, part_width), part_width)
        part = piece[...]
        attended_ref[:, columns] = part
        stream = (patches_ref[:, columns].astype(F32) + part.astype(F32)).astype(BF)
        stream_ref[:, columns] = stream
        stream_f = stream.astype(F32)
        total += jnp.sum(stream_f * stream_f, axis=-1, keepdims=True)
    factor = lax.rsqrt(total / stream_ref.shape[1] + 1e-05)
    normed_ref[...] = (stream_ref[...].astype(F32) * factor * gain_ref[...]).astype(BF)


def residual_norm(me, pieces, patches, gain):
    rows, width = patches.shape
    tile = math.gcd(rows, 32)
    at = lambda step: (step, 0)
    whole = pl.BlockSpec((tile, width), at)
    return pl.pallas_call(
        norm_kernel,
        grid=(rows // tile,),
        in_specs=[pl.BlockSpec(memory_space=pltpu.SMEM)]
        + [pl.BlockSpec((tile, piece.shape[1]), at) for piece in pieces]
        + [whole, pl.BlockSpec((1, width), lambda step: (0, 0))],
        out_specs=[whole] * 3,
        out_shape=[pltpu.HBM((rows, width), BF)] * 2 + [jax.ShapeDtypeStruct((rows, width), BF)],
        compiler_params=pltpu.CompilerParams(vmem_limit_bytes=8 << 20),
    )(me, *pieces, patches, gain)


def routing(expert_ids, gate_levels, first, experts, capacity):
    rows = expert_ids.shape[0]
    routed = expert_ids.reshape(-1)
    names = lax.broadcasted_iota(jnp.int32, (2 * rows, 2 * rows), 1)
    same = (routed[:, None] == routed[None, :]) & (
        names < lax.broadcasted_iota(jnp.int32, (2 * rows, 2 * rows), 0)
    )
    slot = jnp.sum(same.astype(jnp.int32), axis=1)
    local = routed - first
    position = jnp.where((local >= 0) & (local < experts), local * capacity + slot, -1)
    position = position.reshape(rows, 2)
    levels = gate_levels.astype(F32)
    share = levels / jnp.sum(levels, axis=-1, keepdims=True)
    places = lax.broadcasted_iota(jnp.int32, (rows, experts * capacity), 1)
    hit0 = places == position[:, 0:1]
    hit1 = places == position[:, 1:2]
    send = (hit0 | hit1).astype(BF)
    weight = jnp.where(hit0, share[:, 0:1], F32(0)) + jnp.where(hit1, share[:, 1:2], F32(0))
    high = lax.reduce_precision(weight, 8, 7)
    return send, high.astype(BF), (weight - high).astype(BF)


def spread(send, rows):
    return lax.dot_general(
        send, rows, (((0,), (0,)), ((), ())), preferred_element_type=F32
    ).astype(BF)


def gather_back(high, low, rows):
    return jnp.dot(high, rows, preferred_element_type=F32) + jnp.dot(
        low, rows, preferred_element_type=F32
    )


def finish_kernel(high_ref, low_ref, back_ref, stream_ref, other_ref, out_hbm, out_ref, left):
    tile = out_ref.shape[1] // left.shape[0]
    writes = []
    for index in range(left.shape[0]):
        columns = slice(index * tile, (index + 1) * tile)
        mixture = gather_back(high_ref[...], low_ref[...], back_ref[:, columns])
        mixture = mixture + other_ref[:, columns].astype(F32)
        out_ref[:, columns] = (stream_ref[:, columns].astype(F32) + mixture).astype(BF)
        columns = pl.ds(index * tile, tile)
        write = pltpu.make_async_copy(out_ref.at[:, columns], out_hbm.at[:, columns], left.at[index])
        write.start()
        writes.append(write)
    for write in writes:
        write.wait()


def finish(high, low, back, stream, other):
    rows, width = stream.shape
    vmem = pl.BlockSpec(memory_space=pltpu.VMEM)
    return pl.pallas_call(
        finish_kernel,
        in_specs=[vmem] * 5,
        out_specs=pl.BlockSpec(memory_space=pltpu.HBM),
        out_shape=pltpu.HBM((rows, width), BF),
        scratch_shapes=[
            pltpu.VMEM((rows, width), BF),
            pltpu.SemaphoreType.DMA((math.gcd(width // 256, 4),)),
        ],
        compiler_params=pltpu.CompilerParams(vmem_limit_bytes=16 << 20),
    )(high, low, back, stream, other)


def shards(projected, patches, norm_gain, expert_ids, gate_levels, w_gate, w_up, w_down):
    seq_count = lax.axis_size(SEQ)
    half_count = lax.axis_size(HALF)
    lo_count = lax.axis_size("lo")
    tok_rows = patches.shape[1]
    local_heads = HEADS // seq_count
    expert_count = 2 * half_count
    capacity = max(2, 4 * tok_rows // expert_count)
    turned = [(i + lo_count // 2) % lo_count for i in range(lo_count)]
    mirror = [
        (i, (1 - i // lo_count) * lo_count + turned[i % lo_count]) for i in range(seq_count)
    ]
    first = lax.axis_index("hi") * half_count

    def across(value):
        return lax.ppermute(value, SEQ, mirror)

    def swap(turn, value):
        return lax.ppermute(value, SEQ, [(i, i ^ turn) for i in range(seq_count)])

    def exchange(axes, value):
        return lax.all_to_all(value, axes, split_axis=0, concat_axis=0, tiled=True)

    def routed(value):
        sent = value.reshape(half_count, capacity, value.shape[1])
        return exchange(HALF, sent).reshape(value.shape)

    other = across(jnp.concatenate([expert_ids[0], gate_levels[0]], axis=1))
    me = lax.axis_index(SEQ)[None]
    arrived = list(regroup(me, jnp.transpose(projected[0], (1, 0, 2)), seq_count))
    for turn in turns(seq_count):
        arrived[turn] = swap(turn, arrived[turn])
    own_send, own_high, own_low = routing(
        expert_ids[0], gate_levels[0], first, half_count, capacity
    )
    other_send, other_high, other_low = routing(
        other[:, :2], other[:, 2:], first, half_count, capacity
    )
    arrived, own_send, own_high, own_low, other_send, other_high, other_low = (
        lax.optimization_barrier(
            (arrived, own_send, own_high, own_low, other_send, other_high, other_low)
        )
    )
    returned = list(attention(me, arrived, local_heads))
    for turn in turns(seq_count):
        returned[turn] = swap(turn, returned[turn])
    attended, stream, normed = residual_norm(
        me, returned, patches[0], norm_gain[None]
    )

    other_normed = across(normed)
    own_rows = routed(spread(own_send, normed))
    other_rows = routed(spread(other_send, other_normed))
    own_out = expert_ffn(own_rows, w_gate, w_up, w_down)
    other_out = expert_ffn(other_rows, w_gate, w_up, w_down)
    other_back = routed(other_out)
    other_part = across(gather_back(other_high, other_low, other_back).astype(BF))
    own_back = routed(own_out)
    layer_out = finish(own_high, own_low, own_back, stream, other_part)
    return (attended[None], layer_out[None])


def solution(mesh):
    seq_count, exp_count = mesh.shape["seq"], mesh.shape["exp"]
    finer = Mesh(
        mesh.devices.reshape(2, seq_count // 2, exp_count), ("hi", "lo", "exp")
    )
    tokens = P("exp", SEQ)
    experts = P(("hi", "lo", "exp"), None, None)
    return jax.shard_map(
        shards,
        mesh=finer,
        in_specs=(tokens, tokens, P(), tokens, tokens, experts, experts, experts),
        out_specs=(tokens, tokens),
        check_vma=False,
    )
```

```python
import functools
import math

import jax
import jax.numpy as jnp
from jax import lax
from jax.experimental import pallas as pl
from jax.experimental.pallas import tpu as pltpu
from jax.sharding import Mesh
from jax.sharding import PartitionSpec as P


HEADS = 32
SEQ = ("hi", "lo")
HALF = ("lo", "exp")
BF = jnp.bfloat16
F32 = jnp.float32


def turns(count):
    return [*range(count - 2, 0, -1), count - 1]


def attention_kernel(step_rows, me_ref, *refs):
    *refs, qkv_ref, mixed_ref = refs
    blocks, _, rows, head_width = qkv_ref.shape
    pieces, out_refs = refs[:blocks], refs[blocks:]
    for turn, piece in enumerate(pieces):
        qkv_ref[jnp.bitwise_xor(me_ref[0], turn)] = piece[...]
    length = blocks * rows
    factor = math.log2(math.e) / math.sqrt(head_width)
    queries = qkv_ref[:, 0].reshape(length, head_width)
    keys = qkv_ref[:, 1].reshape(length, head_width)
    values = qkv_ref[:, 2].reshape(length, head_width).T
    over_width = (((1,), (1,)), ((), ()))
    shape = (step_rows, step_rows)
    seen = lax.broadcasted_iota(jnp.int32, shape, 0) <= lax.broadcasted_iota(jnp.int32, shape, 1)
    half = step_rows // 2
    starts = range(0, length, step_rows)
    scores = []
    for start in starts:
        middle, stop = start + half, start + step_rows
        part = queries[start:stop]
        pieces = [
            lax.dot_general(keys[start:middle], part, over_width, preferred_element_type=F32),
            lax.dot_general(
                keys[middle:stop], part[half:], over_width, preferred_element_type=F32
            ),
        ]
        pieces[0] = jnp.where(seen[:half], pieces[0], F32(-1e30))
        pieces[1] = jnp.where(seen[:half, :half], pieces[1], F32(-1e30))
        if start:
            pieces.append(
                lax.dot_general(keys[:start], part, over_width, preferred_element_type=F32)
            )
        scores.append(pieces)
    for start, (near, last, *far) in zip(starts, scores):
        middle, stop = start + half, start + step_rows
        highest = jnp.max(near, axis=0, keepdims=True)
        for piece in far:
            highest = jnp.maximum(highest, jnp.max(piece, axis=0, keepdims=True))
        high_last = jnp.maximum(highest[:, half:], jnp.max(last, axis=0, keepdims=True))
        highest = jnp.concatenate([highest[:, :half], high_last], axis=1)
        near = jnp.exp2((near - highest) * factor)
        total = jnp.sum(near, axis=0, keepdims=True)
        mixed = jnp.dot(values[:, start:middle], near.astype(BF), preferred_element_type=F32)
        for piece in far:
            piece = jnp.exp2((piece - highest) * factor)
            total += jnp.sum(piece, axis=0, keepdims=True)
            mixed += jnp.dot(values[:, :start], piece.astype(BF), preferred_element_type=F32)
        last = jnp.exp2((last - high_last) * factor)
        total_last = total[:, half:] + jnp.sum(last, axis=0, keepdims=True)
        mixed_last = mixed[:, half:] + jnp.dot(
            values[:, middle:stop], last.astype(BF), preferred_element_type=F32
        )
        mixed = jnp.concatenate(
            [mixed[:, :half] / total[:, :half], mixed_last / total_last], axis=1
        )
        mixed = mixed.T.astype(BF)
        for block in range(start // rows, stop // rows):
            low = block * rows - start
            mixed_ref[block] = mixed[low : low + rows]
    for turn, out_ref in enumerate(out_refs):
        out_ref[...] = mixed_ref[jnp.bitwise_xor(me_ref[0], turn)]


def attention(me, pieces, local_heads):
    blocks = len(pieces)
    _, rows, local_width = pieces[0].shape
    head_width = local_width // local_heads
    length = blocks * rows
    piece = pl.BlockSpec((3, rows, head_width), lambda head: (0, 0, head))
    return pl.pallas_call(
        functools.partial(attention_kernel, 4 * rows),
        grid=(local_heads,),
        in_specs=[pl.BlockSpec(memory_space=pltpu.SMEM)] + [piece] * blocks,
        out_specs=[pl.BlockSpec((rows, head_width), lambda head: (0, head))] * blocks,
        out_shape=[pltpu.HBM((rows, local_width), BF)] * blocks,
        scratch_shapes=[
            pltpu.VMEM((blocks, 3, rows, head_width), BF),
            pltpu.VMEM((blocks, rows, head_width), BF),
        ],
        compiler_params=pltpu.CompilerParams(vmem_limit_bytes=20 << 20),
        cost_estimate=pl.CostEstimate(
            flops=2 * length * length * local_width,
            bytes_accessed=8 * length * local_width,
            transcendentals=length * length * local_heads // 2,
        ),
    )(me, *pieces)


def expert_kernel(rows_hbm, gate_hbm, up_hbm, down_hbm, out_hbm, rows_ref, gate_ref, up_ref, down_ref, gate_total, up_total, out_ref, arrived, left):
    pieces = arrived.shape[1]

    def read(kind, source, target, piece):
        depth = target.shape[0] // pieces
        part = pl.ds(piece * depth, depth)
        return pltpu.make_async_copy(source.at[0, part], target.at[part], arrived.at[kind, piece])

    gates = [read(0, gate_hbm, gate_ref, piece) for piece in range(pieces)]
    ups = [read(1, up_hbm, up_ref, piece) for piece in range(pieces)]
    downs = [read(2, down_hbm, down_ref, piece) for piece in range(pieces)]
    depth = gate_ref.shape[0] // pieces
    rows = []
    for piece in range(pieces):
        part = pl.ds(piece * depth, depth)
        rows.append(
            pltpu.make_async_copy(
                rows_hbm.at[:, part], rows_ref.at[:, part], arrived.at[3, piece]
            )
        )
    for group in zip(rows, gates, ups):
        for copy in group:
            copy.start()
    for copy in downs:
        copy.start()

    for piece in range(pieces):
        part = slice(piece * depth, (piece + 1) * depth)
        rows[piece].wait()
        for copy, weight, total in (
            (gates[piece], gate_ref, gate_total),
            (ups[piece], up_ref, up_total),
        ):
            copy.wait()
            term = jnp.dot(rows_ref[:, part], weight[part], preferred_element_type=F32)
            total[...] = total[...] + term if piece else term
    gate = gate_total[...]
    hidden = (gate / (1.0 + jnp.exp(-gate)) * up_total[...]).astype(BF)
    for copy in downs:
        copy.wait()
    width = out_ref.shape[1]
    tile = width // left.shape[0]
    writes = []
    for index in range(left.shape[0]):
        columns = slice(index * tile, (index + 1) * tile)
        out_ref[:, columns] = jnp.dot(
            hidden, down_ref[:, columns], preferred_element_type=F32
        ).astype(BF)
        columns = pl.ds(index * tile, tile)
        write = pltpu.make_async_copy(out_ref.at[:, columns], out_hbm.at[:, columns], left.at[index])
        write.start()
        writes.append(write)
    for write in writes:
        write.wait()


def in_hbm(array):
    return pltpu.with_memory_space_constraint(array, pltpu.HBM)


def expert_ffn(rows, w_gate, w_up, w_down):
    count, width = rows.shape
    hidden = w_gate.shape[2]
    hbm = pl.BlockSpec(memory_space=pltpu.HBM)
    pieces = math.gcd(width // 256, 4)
    return pl.pallas_call(
        expert_kernel,
        in_specs=[pl.BlockSpec(memory_space=pl.ANY), hbm, hbm, hbm],
        out_specs=hbm,
        out_shape=pltpu.HBM((count, width), BF),
        scratch_shapes=[
            pltpu.VMEM((count, width), BF),
            pltpu.VMEM((width, hidden), BF),
            pltpu.VMEM((width, hidden), BF),
            pltpu.VMEM((hidden, width), BF),
            pltpu.VMEM((count, hidden), F32),
            pltpu.VMEM((count, hidden), F32),
            pltpu.VMEM((count, width), BF),
            pltpu.SemaphoreType.DMA((4, pieces)),
            pltpu.SemaphoreType.DMA((2 * pieces,)),
        ],
        compiler_params=pltpu.CompilerParams(vmem_limit_bytes=32 << 20),
        cost_estimate=pl.CostEstimate(
            flops=6 * count * width * hidden,
            bytes_accessed=6 * width * hidden + 4 * count * width,
            transcendentals=count * hidden,
        ),
    )(rows, in_hbm(w_gate), in_hbm(w_up), in_hbm(w_down))


def regroup_kernel(chosen, me_ref, in_ref, *refs):
    *out_refs, held, arrived, left = refs
    _, _, _, local_width = held.shape
    reads, writes = [], []
    for index, (turn, out_ref) in enumerate(zip(chosen, out_refs)):
        block = jnp.bitwise_xor(me_ref[0], turn)
        columns = pl.ds(pl.multiple_of(block * local_width, local_width), local_width)
        reads.append(
            pltpu.make_async_copy(in_ref.at[:, :, columns], held.at[index], arrived.at[index])
        )
        writes.append(pltpu.make_async_copy(held.at[index], out_ref, left.at[index]))
    for read in reads:
        read.start()
    for read, write in zip(reads, writes):
        read.wait()
        write.start()
    for write in writes:
        write.wait()


def regroup(me, projected, blocks, chosen):
    kinds, rows, width = projected.shape
    shape = (kinds, rows, width // blocks)
    blocks = len(chosen)
    hbm = pl.BlockSpec(memory_space=pltpu.HBM)
    return pl.pallas_call(
        functools.partial(regroup_kernel, chosen),
        in_specs=[pl.BlockSpec(memory_space=pltpu.SMEM), hbm],
        out_specs=[hbm] * blocks,
        out_shape=[pltpu.HBM(shape, BF)] * blocks,
        scratch_shapes=[
            pltpu.VMEM((blocks,) + shape, BF),
            pltpu.SemaphoreType.DMA((blocks,)),
            pltpu.SemaphoreType.DMA((blocks,)),
        ],
        compiler_params=pltpu.CompilerParams(vmem_limit_bytes=59 << 20),
    )(me, projected)


def norm_kernel(me_ref, *refs):
    *pieces, patches_ref, gain_ref, attended_ref, stream_ref, normed_ref = refs
    part_width = pieces[0].shape[1]
    total = 0.0
    for turn, piece in enumerate(pieces):
        block = jnp.bitwise_xor(me_ref[0], turn)
        columns = pl.ds(pl.multiple_of(block * part_width, part_width), part_width)
        part = piece[...]
        attended_ref[:, columns] = part
        stream = (patches_ref[:, columns].astype(F32) + part.astype(F32)).astype(BF)
        stream_ref[:, columns] = stream
        stream_f = stream.astype(F32)
        total += jnp.sum(stream_f * stream_f, axis=-1, keepdims=True)
    factor = lax.rsqrt(total / stream_ref.shape[1] + 1e-05)
    normed_ref[...] = (stream_ref[...].astype(F32) * factor * gain_ref[...]).astype(BF)


def residual_norm(me, pieces, patches, gain):
    rows, width = patches.shape
    tile = math.gcd(rows, 32)
    at = lambda step: (step, 0)
    whole = pl.BlockSpec((tile, width), at)
    return pl.pallas_call(
        norm_kernel,
        grid=(rows // tile,),
        in_specs=[pl.BlockSpec(memory_space=pltpu.SMEM)]
        + [pl.BlockSpec((tile, piece.shape[1]), at) for piece in pieces]
        + [whole, pl.BlockSpec((1, width), lambda step: (0, 0))],
        out_specs=[whole] * 3,
        out_shape=[pltpu.HBM((rows, width), BF)] * 2 + [jax.ShapeDtypeStruct((rows, width), BF)],
        compiler_params=pltpu.CompilerParams(vmem_limit_bytes=8 << 20),
    )(me, *pieces, patches, gain)


def routing(expert_ids, gate_levels, first, experts, capacity):
    rows = expert_ids.shape[0]
    routed = expert_ids.reshape(-1)
    names = lax.broadcasted_iota(jnp.int32, (2 * rows, 2 * rows), 1)
    same = (routed[:, None] == routed[None, :]) & (
        names < lax.broadcasted_iota(jnp.int32, (2 * rows, 2 * rows), 0)
    )
    slot = jnp.sum(same.astype(jnp.int32), axis=1)
    local = routed - first
    position = jnp.where((local >= 0) & (local < experts), local * capacity + slot, -1)
    position = position.reshape(rows, 2)
    levels = gate_levels.astype(F32)
    share = levels / jnp.sum(levels, axis=-1, keepdims=True)
    places = lax.broadcasted_iota(jnp.int32, (rows, experts * capacity), 1)
    hit0 = places == position[:, 0:1]
    hit1 = places == position[:, 1:2]
    send = (hit0 | hit1).astype(BF)
    weight = jnp.where(hit0, share[:, 0:1], F32(0)) + jnp.where(hit1, share[:, 1:2], F32(0))
    high = lax.reduce_precision(weight, 8, 7)
    return send, high.astype(BF), (weight - high).astype(BF)


def spread(send, rows):
    return lax.dot_general(
        send, rows, (((0,), (0,)), ((), ())), preferred_element_type=F32
    ).astype(BF)


def gather_back(high, low, rows):
    return jnp.dot(high, rows, preferred_element_type=F32) + jnp.dot(
        low, rows, preferred_element_type=F32
    )


def finish_kernel(high_ref, low_ref, back_ref, stream_ref, other_ref, out_hbm, out_ref, left):
    tile = out_ref.shape[1] // left.shape[0]
    writes = []
    for index in range(left.shape[0]):
        columns = slice(index * tile, (index + 1) * tile)
        mixture = gather_back(high_ref[...], low_ref[...], back_ref[:, columns])
        mixture = mixture + other_ref[:, columns].astype(F32)
        out_ref[:, columns] = (stream_ref[:, columns].astype(F32) + mixture).astype(BF)
        columns = pl.ds(index * tile, tile)
        write = pltpu.make_async_copy(out_ref.at[:, columns], out_hbm.at[:, columns], left.at[index])
        write.start()
        writes.append(write)
    for write in writes:
        write.wait()


def finish(high, low, back, stream, other):
    rows, width = stream.shape
    vmem = pl.BlockSpec(memory_space=pltpu.VMEM)
    return pl.pallas_call(
        finish_kernel,
        in_specs=[vmem] * 5,
        out_specs=pl.BlockSpec(memory_space=pltpu.HBM),
        out_shape=pltpu.HBM((rows, width), BF),
        scratch_shapes=[
            pltpu.VMEM((rows, width), BF),
            pltpu.SemaphoreType.DMA((math.gcd(width // 256, 4),)),
        ],
        compiler_params=pltpu.CompilerParams(vmem_limit_bytes=16 << 20),
    )(high, low, back, stream, other)


def shards(projected, patches, norm_gain, expert_ids, gate_levels, w_gate, w_up, w_down):
    seq_count = lax.axis_size(SEQ)
    half_count = lax.axis_size(HALF)
    lo_count = lax.axis_size("lo")
    tok_rows = patches.shape[1]
    local_heads = HEADS // seq_count
    expert_count = 2 * half_count
    capacity = max(2, 4 * tok_rows // expert_count)
    turned = [(i + lo_count // 2) % lo_count for i in range(lo_count)]
    mirror = [
        (i, (1 - i // lo_count) * lo_count + turned[i % lo_count]) for i in range(seq_count)
    ]
    first = lax.axis_index("hi") * half_count

    def across(value):
        return lax.ppermute(value, SEQ, mirror)

    def swap(turn, value):
        return lax.ppermute(value, SEQ, [(i, i ^ turn) for i in range(seq_count)])

    def exchange(axes, value):
        return lax.all_to_all(value, axes, split_axis=0, concat_axis=0, tiled=True)

    def routed(value):
        sent = value.reshape(half_count, capacity, value.shape[1])
        return exchange(HALF, sent).reshape(value.shape)

    other = across(jnp.concatenate([expert_ids[0], gate_levels[0]], axis=1))
    me = lax.axis_index(SEQ)[None]
    kinds = jnp.transpose(projected[0], (1, 0, 2))
    first_turn, *later = turns(seq_count)
    later = tuple(later) + (0,)
    (head,) = regroup(me, kinds, seq_count, (first_turn,))
    rest = regroup(me, kinds, seq_count, later)
    arrived = {turn: piece for turn, piece in zip((first_turn,) + later, (head, *rest))}
    arrived = [swap(turn, arrived[turn]) if turn else arrived[turn] for turn in range(seq_count)]
    own_send, own_high, own_low = routing(
        expert_ids[0], gate_levels[0], first, half_count, capacity
    )
    other_send, other_high, other_low = routing(
        other[:, :2], other[:, 2:], first, half_count, capacity
    )
    arrived, own_send, own_high, own_low, other_send, other_high, other_low = (
        lax.optimization_barrier(
            (arrived, own_send, own_high, own_low, other_send, other_high, other_low)
        )
    )
    returned = list(attention(me, arrived, local_heads))
    for turn in turns(seq_count):
        returned[turn] = swap(turn, returned[turn])
    attended, stream, normed = residual_norm(
        me, returned, patches[0], norm_gain[None]
    )

    other_normed = across(normed)
    own_rows = routed(spread(own_send, normed))
    other_rows = routed(spread(other_send, other_normed))
    own_out = expert_ffn(own_rows, w_gate, w_up, w_down)
    other_out = expert_ffn(other_rows, w_gate, w_up, w_down)
    other_back = routed(other_out)
    other_part = across(gather_back(other_high, other_low, other_back).astype(BF))
    own_back = routed(own_out)
    layer_out = finish(own_high, own_low, own_back, stream, other_part)
    return (attended[None], layer_out[None])


def solution(mesh):
    seq_count, exp_count = mesh.shape["seq"], mesh.shape["exp"]
    finer = Mesh(
        mesh.devices.reshape(2, seq_count // 2, exp_count), ("hi", "lo", "exp")
    )
    tokens = P("exp", SEQ)
    experts = P(("hi", "lo", "exp"), None, None)
    return jax.shard_map(
        shards,
        mesh=finer,
        in_specs=(tokens, tokens, P(), tokens, tokens, experts, experts, experts),
        out_specs=(tokens, tokens),
        check_vma=False,
    )
```
